256 devices in a mesh: tm: 8 (over z), tile: 32 (over y, x, core).
Axes of the slice: x: 4, y: 4, z: 8, core: 2. Of those that a mesh axis runs over, the one named last changes fastest.
Arguments:
- heads: float32 [8, 3, 512, 4096], P('tm', None, 'tile'), may hold values from -6 to 6
- capacity: float32 [512, 4096], P('tile'), may hold values from 0.5 to 2
- cond_row: float32 [512, 4096], P('tile'), may hold values from 0.1 to 1
- cond_col: float32 [512, 4096], P('tile'), may hold values from 0.1 to 1
- terminal: float32 [2, 512, 4096], P(None, 'tile'), may hold values from -6 to 6
- obs_cell: int32 [8, 2, 512], P('tm'), may hold values from 0 to 2097151
- obs_weight: float32 [8, 2, 2, 512], P('tm'), may hold values from -8 to 8
- block_mask: int32 [4, 32], replicated, may hold values 0 or 1
Outputs:
- adjoint_start: float32 [8, 2, 512, 4096], P('tm', None, 'tile')
- cond_sens: float32 [512, 4096], P('tile', 'tm')
- storage_sens: float32 [2], replicated
The draws below stay inside these ranges and needn't reach their ends.
Inputs may be any that keep to these rules, and one draw needn't show every extreme that they name: `obs_cell`: row * 4096 + column of an observed cell; a cell may repeat.
All inputs are finite; a program needn't handle non-finite values.
Results may differ from the reference program's by a relative error of at most 0.0003.
Values sent between devices are 32-bit elements; how exact they have to be, the bound alone decides.
A program may use at most 64 MiB of HBM per device.

```python
import math
import jax
import jax.numpy as jnp

NY = 4096
BLOCK = 128
MEMBERS = 2
NOBS = 512
STEPS = 2
SWEEPS = 2
SECTIONS = 8
NX = 512


def with_ends(values, rng, least, top_value):
    spot = [jax.random.randint(jax.random.fold_in(rng, axis), (), 0, length) for axis, length in enumerate(values.shape)]
    widest = values.shape.index(max(values.shape))
    neighbour = spot[:widest] + [(spot[widest] + 1) % values.shape[widest]] + spot[widest + 1:]
    return values.at[tuple(spot)].set(least).at[tuple(neighbour)].set(top_value)


def steps_of(own_key, extent, cuts, least, high):
    def one(dim, shards_of):
        steps = jax.random.uniform(jax.random.fold_in(jax.random.fold_in(own_key, 6), dim), (shards_of,), jnp.float32, least / len(cuts), high / len(cuts))
        return jnp.repeat(jnp.exp(steps), extent[dim] // shards_of).reshape((-1,) + (1,) * (len(extent) - dim - 1))

    gain = one(*cuts[0])
    for cut in cuts[1:]:
        gain = gain * one(*cut)
    return gain


def bell_draw(rng, dims, width, limit, pieces=(), kind=jnp.bfloat16):
    result = width * jax.random.normal(rng, dims, jnp.float32)
    if pieces:
        result = result * steps_of(rng, dims, pieces, -0.22, 0.18)
    return jnp.clip(result, -limit, limit).astype(kind)


def setup_inputs(seed: int = 0) -> dict:
    streams_of = jax.random.split(jax.random.key(seed), 9)
    heads = bell_draw(streams_of[0], (SECTIONS, STEPS + 1, NX, NY), 1.0, 6.0, ((0, 8), (2, 32)), jnp.float32)
    capacity = jnp.clip(jnp.exp(math.log(2.0) - 1.3862944 * jax.random.uniform(streams_of[1], (NX, NY), jnp.float32) ** steps_of(streams_of[1], (NX, NY), ((0, 32),), -0.2, 0.2)), 0.5, 2.0)
    cond_row = jnp.clip(jnp.exp(math.log(1.0) - 2.3025851 * jax.random.uniform(streams_of[2], (NX, NY), jnp.float32) ** steps_of(streams_of[2], (NX, NY), ((0, 32),), -0.2, 0.2)), 0.1, 1.0)
    cond_col = jnp.clip(jnp.exp(math.log(1.0) - 2.3025851 * jax.random.uniform(streams_of[3], (NX, NY), jnp.float32) ** steps_of(streams_of[3], (NX, NY), ((0, 32),), -0.2, 0.2)), 0.1, 1.0)
    terminal = bell_draw(streams_of[4], (MEMBERS, NX, NY), 1.0, 6.0, ((1, 32),), jnp.float32)
    obs_cell = with_ends(jax.random.randint(streams_of[5], (SECTIONS, STEPS, NOBS), 0, NX * NY), jax.random.fold_in(streams_of[5], 1), 0, (NX * NY) - 1).astype(jnp.int32)
    obs_weight = bell_draw(streams_of[6], (SECTIONS, STEPS, MEMBERS, NOBS), 2.0, 8.0, ((0, 8),), jnp.float32)
    block_mask = with_ends((jax.random.randint(streams_of[7], (NX // BLOCK, NY // BLOCK), 0, 4) < 3).astype(jnp.int32), jax.random.fold_in(streams_of[7], 1), 0, 1)
    return {"heads": heads, "capacity": capacity, "cond_row": cond_row, "cond_col": cond_col, "terminal": terminal, "obs_cell": obs_cell, "obs_weight": obs_weight, "block_mask": block_mask}


def relax(field, rhs, east, west, south, north, diagonal):
    padded = jnp.pad(field, ((0, 0), (1, 1), (1, 1)))
    above = padded[:, :-2, 1:-1]
    below = padded[:, 2:, 1:-1]
    left = padded[:, 1:-1, :-2]
    right = padded[:, 1:-1, 2:]
    return (rhs + east * right + west * left + south * below + north * above) / diagonal


def reference(heads, capacity, cond_row, cond_col, terminal, obs_cell, obs_weight, block_mask):
    active = jnp.repeat(jnp.repeat(block_mask.astype(jnp.float32), BLOCK, axis=0), BLOCK, axis=1)
    zero_col = jnp.zeros((NX, 1), jnp.float32)
    zero_row = jnp.zeros((1, NY), jnp.float32)
    pair = active * jnp.concatenate([active[:, 1:], zero_col], axis=1)
    east = cond_row * pair
    west = jnp.concatenate([zero_col, east[:, :-1]], axis=1)
    next_active = jnp.concatenate([active[1:], zero_row], axis=0)
    south = cond_col * active * next_active
    north = jnp.concatenate([zero_row, south[:-1]], axis=0)
    diagonal = capacity + east + west + south + north
    field = terminal
    starts = []
    sens = jnp.zeros((NX, NY), jnp.float32)
    storage = jnp.zeros((MEMBERS,), jnp.float32)
    zero_cols = jnp.zeros((MEMBERS, NX, 1), jnp.float32)
    for section in reversed(range(SECTIONS)):
        for step in reversed(range(STEPS)):
            cells = obs_cell[section, step]
            cell_row = cells // NY
            cell_col = cells % NY
            force = jnp.zeros((MEMBERS, NX, NY), jnp.float32).at[:, cell_row, cell_col].add(obs_weight[section, step])
            rhs = active * (capacity * field + force)
            for sweep_index in range(SWEEPS):
                field = relax(field, rhs, east, west, south, north, diagonal)
            later = heads[section, step + 1]
            earlier = heads[section, step]
            head_step = jnp.concatenate([later[:, 1:] - later[:, :-1], zero_col], axis=1)
            adj_step = jnp.concatenate([field[:, :, 1:] - field[:, :, :-1], zero_cols], axis=2)
            sens = sens + jnp.sum(adj_step * head_step * pair, axis=0)
            storage = storage + jnp.sum(field * capacity * (later - earlier), axis=(1, 2))
        starts.insert(0, field)
    return jnp.stack(starts), sens, storage
```

```python
import functools

import jax
import jax.numpy as jnp
from jax import lax
from jax.experimental import pallas as pl
from jax.experimental.pallas import tpu as pltpu
from jax.sharding import PartitionSpec as P

STEPS = 2
LANES = 128
MESH = pl.DeviceIdType.MESH


def kernel(cfg, heads, cap, crow, ccol, term, ocell, oweight, mask, out_a, out_c, out_s,
           ext, field, mid, rhs, coef, force, cells, weights, head, saved, red_a, red_b, red_c,
           loc_sem, halo_send, halo_recv, obs_send, obs_recv, head_send, head_recv,
           mid_send, mid_recv, start_send, start_recv, red_send, red_recv):
    planes, tiles, inner, rows, cols, total_cols, block_rows, block_cols = cfg
    wide = cols + 2 * LANES
    tall = 3 * rows
    edge = cols + LANES
    total_rows = rows * tiles
    me = lax.axis_index("tm")
    tile = lax.axis_index("tile")
    above = lax.rem(tile + tiles - 1, tiles)
    below = lax.rem(tile + 1, tiles)
    group = tile // inner
    place = lax.rem(tile, inner)
    outer = tiles // inner

    def plane_at(d):
        return lax.rem(me + d, planes)

    def inner_at(d):
        return group * inner + lax.rem(place + d, inner)

    def outer_at(d):
        return lax.rem(group + d, outer) * inner + place

    def at(plane, row_tile):
        return {"tm": plane, "tile": row_tile}

    partners = [(plane_at(d), tile) for d in range(1, planes)]
    partners += [(me, above), (me, below)]
    partners += [(me, inner_at(d)) for d in range(1, inner)]
    partners += [(me, outer_at(d)) for d in range(1, outer)]
    barrier = pltpu.get_barrier_semaphore()
    for plane, row_tile in partners:
        pl.semaphore_signal(barrier, inc=1, device_id=at(plane, row_tile), device_id_type=MESH)

    def lane(offset):
        return pl.multiple_of(lax.rem(offset + total_cols, total_cols), LANES)

    first = me * cols
    pieces = [
        (lane(first - LANES), LANES, 0),
        (lane(first), cols, LANES),
        (lane(first + cols), LANES, LANES + cols),
    ]

    def own_parts(row):
        parts = []
        for start, size, to in pieces:
            for i, ref in enumerate((cap, crow, ccol)):
                parts.append((ref.at[:, pl.ds(start, size)],
                              ext.at[i, pl.ds(row, rows), pl.ds(to, size)]))
            parts.append((term.at[:, :, pl.ds(start, size)],
                          field.at[0, :, pl.ds(row, rows), pl.ds(to, size)]))
        return parts

    def head_parts(target, source):
        begin = lane(target * cols)
        after = lane(target * cols + cols)
        return [
            (heads.at[0, :, :, pl.ds(begin, cols)], head.at[source, :, :, pl.ds(0, cols)]),
            (heads.at[0, pl.ds(1, 2), :, pl.ds(after, LANES)],
             head.at[source, pl.ds(1, 2), :, pl.ds(cols, LANES)]),
        ]

    def obs_parts(source):
        return [(ocell.at[0], cells.at[source]), (oweight.at[0], weights.at[source])]

    local = []
    for src, dst in own_parts(rows) + head_parts(me, me) + obs_parts(me):
        copy = pltpu.make_async_copy(src, dst, loc_sem.at[len(local)])
        copy.start()
        local.append(copy)
    pl.semaphore_wait(barrier, len(partners))

    def remote(src, dst, send, recv, plane, row_tile):
        return pltpu.make_async_remote_copy(
            src_ref=src, dst_ref=dst, send_sem=send, recv_sem=recv,
            device_id=at(plane, row_tile), device_id_type=MESH)

    def obs_copies(d, source):
        return [remote(src, dst, obs_send.at[d, i], obs_recv.at[d, i], plane_at(d), tile)
                for i, (src, dst) in enumerate(obs_parts(source))]

    def head_copies(d, source):
        return [remote(src, dst, head_send.at[d, i], head_recv.at[d, i], plane_at(d), tile)
                for i, (src, dst) in enumerate(head_parts(plane_at(d), source))]

    sent = []
    for d in range(1, planes):
        sent += obs_copies(d, me)
    halos = []
    for way, (row, target) in enumerate(((2 * rows, above), (0, below))):
        for i, (src, dst) in enumerate(own_parts(row)):
            halos.append(remote(src, dst, halo_send.at[way, i], halo_recv.at[way, i], me, target))
    order = sorted(range(1, planes), key=lambda d: -min(d, planes - d))
    for copy in sent + halos:
        copy.start()
    sent_heads = []
    for d in order:
        sent_heads += head_copies(d, me)
    for copy in sent_heads:
        copy.start()

    for copy in local:
        copy.wait()
    for d in range(1, planes):
        for copy in obs_copies(d, plane_at(planes - d)):
            copy.wait_recv()

    row_ids = lax.broadcasted_iota(jnp.int32, (tall, 1), 0)
    col_ids = lax.broadcasted_iota(jnp.int32, (wide, 1), 0)

    def forcing(section, carry):
        for step in range(STEPS):
            cell = cells[section, step : step + 1, :]
            cell_row = cell // total_cols
            cell_col = cell - cell_row * total_cols
            near_row = lax.rem(cell_row - tile * rows + rows + total_rows, total_rows)
            near_col = lax.rem(cell_col - me * cols + LANES + total_cols, total_cols)
            row_hit = near_row == row_ids
            col_hit = jnp.where(near_col == col_ids, 1.0, 0.0).astype(jnp.bfloat16)
            parts = []
            for member in range(2):
                rest = weights[section, step, member : member + 1, :]
                for _ in range(3):
                    part = rest.astype(jnp.bfloat16).astype(jnp.float32)
                    rest = rest - part
                    parts.append(jnp.where(row_hit, part, 0.0).astype(jnp.bfloat16))
            stacked = jnp.concatenate(parts, axis=0)
            got = lax.dot_general(stacked, col_hit, (((1,), (1,)), ((), ())),
                                  preferred_element_type=jnp.float32)
            for member in range(2):
                begin = 3 * member * tall
                force[section, step, member] = (
                    got[begin : begin + tall]
                    + got[begin + tall : begin + 2 * tall]
                    + got[begin + 2 * tall : begin + 3 * tall])
        return carry

    lax.fori_loop(0, planes, forcing, 0)

    for copy in halos:
        copy.wait_recv()

    def activity(shift, j):
        row_tile = lax.rem(tile + shift + tiles, tiles)
        block = lax.rem(first - LANES + j * LANES + total_cols, total_cols) // block_cols
        return mask[(row_tile * rows) // block_rows, block].astype(jnp.float32)

    lane_id = lax.broadcasted_iota(jnp.int32, (rows, LANES), 1)
    row_id = lax.broadcasted_iota(jnp.int32, (rows, LANES), 0)
    act_bands, pair_bands, down_bands = [], [], []
    for band in range(3):
        act_row, pair_row, down_row = [], [], []
        last_row = lax.rem(tile + band - 1 + tiles, tiles) == tiles - 1
        for j in range(wide // LANES):
            here = activity(band - 1, j)
            last_col = lax.rem(first + j * LANES + total_cols, total_cols) == 0
            beside = jnp.where(last_col, 0.0, activity(band - 1, j + 1))
            under = jnp.where(last_row, 0.0, activity(band, j))
            act_row.append(jnp.full((rows, LANES), here, jnp.float32))
            pair_row.append(here * jnp.where(lane_id == LANES - 1, beside, here))
            down_row.append(here * jnp.where(row_id == rows - 1, under, here))
        act_bands.append(jnp.concatenate(act_row, axis=1))
        pair_bands.append(jnp.concatenate(pair_row, axis=1))
        down_bands.append(jnp.concatenate(down_row, axis=1))
    pair_core = pair_bands[1][:, LANES : LANES + cols]
    active = jnp.concatenate(act_bands, axis=0)
    east = ext[1] * jnp.concatenate(pair_bands, axis=0)
    south = ext[2] * jnp.concatenate(down_bands, axis=0)
    west = pltpu.roll(east, 1, 1)
    north = pltpu.roll(south, 1, 0)
    capacity = ext[0]
    inverse = 1.0 / (capacity + east + west + south + north)
    coef[0] = east * inverse
    coef[1] = west * inverse
    coef[2] = south * inverse
    coef[3] = north * inverse
    coef[4] = active * capacity * inverse
    coef[5] = active * inverse

    sub_id = lax.broadcasted_iota(jnp.int32, (1, 8, wide), 1)
    strips = tall // 8

    def stencil(source, i):
        start = pl.multiple_of(i * 8, 8)
        before = pl.multiple_of(jnp.maximum(i - 1, 0) * 8, 8)
        after = pl.multiple_of(jnp.minimum(i + 1, strips - 1) * 8, 8)
        here = source[:, pl.ds(start, 8), :]
        up = jnp.where(sub_id == 0, pltpu.roll(source[:, pl.ds(before, 8), :], 1, 1),
                       pltpu.roll(here, 1, 1))
        down = jnp.where(sub_id == 7, pltpu.roll(source[:, pl.ds(after, 8), :], 7, 1),
                         pltpu.roll(here, 7, 1))
        right = pltpu.roll(here, wide - 1, 2)
        left = pltpu.roll(here, 1, 2)
        strip = pl.ds(start, 8)
        total = (coef[0, strip, :][None] * right + coef[1, strip, :][None] * left
                 + coef[2, strip, :][None] * down + coef[3, strip, :][None] * up)
        return here, total, strip

    def one_step(now, section, step):
        def first_sweep(i, carry):
            here, total, strip = stencil(now, i)
            part = (coef[4, strip, :][None] * here
                    + coef[5, strip, :][None] * force[section, step, :, strip, :])
            rhs[:, strip, :] = part
            mid[:, strip, :] = part + total
            return carry

        def second_sweep(i, carry):
            _, total, strip = stencil(mid, i)
            now[:, strip, :] = rhs[:, strip, :] + total
            return carry

        lax.fori_loop(0, strips, first_sweep, 0)
        lax.fori_loop(0, strips, second_sweep, 0)
        saved[section, step] = now[:, rows : 2 * rows, LANES:]

    def start_copy(section, d):
        return remote(saved.at[section, 0, :, :, pl.ds(0, cols)],
                      out_a.at[0, :, :, pl.ds(pl.multiple_of(first, LANES), cols)],
                      start_send.at[d], start_recv.at[d], section, tile)

    def own_start():
        return pltpu.make_async_copy(
            saved.at[me, 0, :, :, pl.ds(0, cols)],
            out_a.at[0, :, :, pl.ds(pl.multiple_of(first, LANES), cols)],
            loc_sem.at[0])

    half = planes // 2
    mids = []
    for phase in range(2):
        now = field.at[phase]

        def one_section(turn, carry):
            section = planes - 1 - phase * half - turn
            for step in reversed(range(STEPS)):
                one_step(now, section, step)
            d = lax.rem(section - me + planes, planes)

            @pl.when(section != me)
            def _():
                start_copy(section, d).start()

            @pl.when(section == me)
            def _():
                own_start().start()

            return carry

        lax.fori_loop(0, half, one_section, 0)
        if phase == 0:
            core = pl.ds(rows, rows)
            field[1, :, rows : 2 * rows, :] = field[0, :, rows : 2 * rows, :]
            for way, (row, target) in enumerate(((2 * rows, above), (0, below))):
                copy = remote(field.at[0, :, core, :], field.at[1, :, pl.ds(row, rows), :],
                              mid_send.at[way], mid_recv.at[way], me, target)
                copy.start()
                mids.append(copy)
            for copy in mids:
                copy.wait_recv()

    for d in range(1, planes):
        for copy in head_copies(d, plane_at(planes - d)):
            copy.wait_recv()

    def sums(section, carry):
        sens, store_0, store_1 = carry
        for step in range(STEPS):
            a_0 = saved[section, step, 0]
            a_1 = saved[section, step, 1]
            later = head[section, step + 1]
            both = a_0 + a_1
            jump = ((pltpu.roll(both, edge - 1, 1) - both)
                    * (pltpu.roll(later, edge - 1, 1) - later))
            sens = sens + jump[:, :cols]
            change = later[:, :cols] - head[section, step, :, pl.ds(0, cols)]
            store_0 = store_0 + a_0[:, :cols] * change
            store_1 = store_1 + a_1[:, :cols] * change
        return sens, store_0, store_1

    zero = jnp.zeros((rows, cols), jnp.float32)
    sens, store_0, store_1 = lax.fori_loop(0, planes, sums, (zero, zero, zero))
    out_c[...] = sens * pair_core
    cap_core = ext[0, rows : 2 * rows, LANES : LANES + cols]
    tile_lane = lax.broadcasted_iota(jnp.int32, (8, LANES), 1)
    part = jnp.where(tile_lane == 0, jnp.sum(store_0 * cap_core), 0.0)
    part = jnp.where(tile_lane == 1, jnp.sum(store_1 * cap_core), part)

    reduce_sends = []

    def exchange(value, slots, place_here, count, partner, base):
        slots[place_here] = value
        copies = []
        for d in range(1, count):
            plane, row_tile = partner(d)
            copies.append(remote(slots.at[place_here], slots.at[place_here],
                                 red_send.at[base + d], red_recv.at[base + d], plane, row_tile))
        for copy in copies:
            copy.start()
        for d in range(1, count):
            source = lax.rem(place_here + count - d, count)
            plane, row_tile = partner(d)
            remote(slots.at[source], slots.at[source], red_send.at[base + d],
                   red_recv.at[base + d], plane, row_tile).wait_recv()
        reduce_sends.extend(copies)
        total = slots[0]
        for i in range(1, count):
            total = total + slots[i]
        return total

    part = exchange(part, red_b, place, inner, lambda d: (me, inner_at(d)), 0)
    part = exchange(part, red_c, group, outer, lambda d: (me, outer_at(d)), inner)
    part = exchange(part, red_a, me, planes, lambda d: (plane_at(d), tile), inner + outer)
    out_s[0] = jnp.sum(jnp.where(tile_lane[:1] == 0, part[:1], 0.0))
    out_s[1] = jnp.sum(jnp.where(tile_lane[:1] == 1, part[:1], 0.0))

    own_start().wait()
    for d in range(1, planes):
        source = plane_at(planes - d)
        remote(saved.at[me, 0, :, :, pl.ds(0, cols)],
               out_a.at[0, :, :, pl.ds(pl.multiple_of(source * cols, LANES), cols)],
               start_send.at[d], start_recv.at[d], plane_at(d), tile).wait_recv()
    for d in range(1, planes):
        start_copy(plane_at(d), d).wait_send()
    for copy in sent + halos + sent_heads + mids + reduce_sends:
        copy.wait_send()


def solution(mesh):
    planes, tiles = mesh.shape["tm"], mesh.shape["tile"]
    inner = min(8, tiles // 2)
    outer = tiles // inner

    def shards(heads, capacity, cond_row, cond_col, terminal, obs_cell, obs_weight, block_mask):
        rows, total_cols = capacity.shape
        cols = total_cols // planes
        wide, tall, edge = cols + 2 * LANES, 3 * rows, cols + LANES
        observed = obs_cell.shape[2]
        block_rows = rows * tiles // block_mask.shape[0]
        block_cols = total_cols // block_mask.shape[1]
        cfg = (planes, tiles, inner, rows, cols, total_cols, block_rows, block_cols)
        f32 = jnp.float32
        dma = pltpu.SemaphoreType.DMA
        any_spec = pl.BlockSpec(memory_space=pl.ANY)
        out = pl.pallas_call(
            functools.partial(kernel, cfg),
            out_shape=(
                jax.ShapeDtypeStruct((1, 2, rows, total_cols), f32),
                jax.ShapeDtypeStruct((rows, cols), f32),
                jax.ShapeDtypeStruct((2,), f32),
            ),
            in_specs=[any_spec] * 7 + [pl.BlockSpec(memory_space=pltpu.SMEM)],
            out_specs=(any_spec, pl.BlockSpec(memory_space=pltpu.VMEM),
                       pl.BlockSpec(memory_space=pltpu.SMEM)),
            scratch_shapes=[
                pltpu.VMEM((3, tall, wide), f32),
                pltpu.VMEM((2, 2, tall, wide), f32),
                pltpu.VMEM((2, tall, wide), f32),
                pltpu.VMEM((2, tall, wide), f32),
                pltpu.VMEM((6, tall, wide), f32),
                pltpu.VMEM((planes, STEPS, 2, tall, wide), f32),
                pltpu.VMEM((planes, STEPS, observed), jnp.int32),
                pltpu.VMEM((planes, STEPS, 2, observed), f32),
                pltpu.VMEM((planes, 3, rows, edge), f32),
                pltpu.VMEM((planes, STEPS, 2, rows, edge), f32),
                pltpu.VMEM((planes, 8, LANES), f32),
                pltpu.VMEM((inner, 8, LANES), f32),
                pltpu.VMEM((outer, 8, LANES), f32),
                dma((16,)),
                dma((2, 12)),
                dma((2, 12)),
                dma((planes, 2)),
                dma((planes, 2)),
                dma((planes, 2)),
                dma((planes, 2)),
                dma((2,)),
                dma((2,)),
                dma((planes,)),
                dma((planes,)),
                dma((planes + inner + outer,)),
                dma((planes + inner + outer,)),
            ],
            compiler_params=pltpu.CompilerParams(
                collective_id=0, has_side_effects=True, vmem_limit_bytes=48 * 1024 * 1024
            ),
        )(heads, capacity, cond_row, cond_col, terminal, obs_cell, obs_weight, block_mask)
        return out

    in_specs = (
        P("tm", None, "tile", None),
        P("tile", None),
        P("tile", None),
        P("tile", None),
        P(None, "tile", None),
        P("tm", None, None),
        P("tm", None, None, None),
        P(),
    )
    out_specs = (P("tm", None, "tile", None), P("tile", "tm"), P())
    return jax.shard_map(
        shards, mesh=mesh, in_specs=in_specs, out_specs=out_specs, check_vma=False
    )
```

```python
import functools

import jax
import jax.numpy as jnp
from jax import lax
from jax.experimental import pallas as pl
from jax.experimental.pallas import tpu as pltpu
from jax.sharding import PartitionSpec as P

STEPS = 2
LANES = 128
MESH = pl.DeviceIdType.MESH


def kernel(cfg, heads, cap, crow, ccol, term, ocell, oweight, mask, out_a, out_c, out_s,
           ext, field, mid, rhs, coef, force, cells, weights, head, saved, red_a, red_b, red_c,
           loc_sem, halo_send, halo_recv, obs_send, obs_recv, head_send, head_recv,
           mid_send, mid_recv, start_send, start_recv, red_send, red_recv):
    planes, tiles, inner, rows, cols, total_cols, block_rows, block_cols = cfg
    wide = cols + 2 * LANES
    tall = 3 * rows
    edge = cols + LANES
    total_rows = rows * tiles
    me = lax.axis_index("tm")
    tile = lax.axis_index("tile")
    above = lax.rem(tile + tiles - 1, tiles)
    below = lax.rem(tile + 1, tiles)
    group = tile // inner
    place = lax.rem(tile, inner)
    outer = tiles // inner

    def plane_at(d):
        return lax.rem(me + d, planes)

    def inner_at(d):
        return group * inner + lax.rem(place + d, inner)

    def outer_at(d):
        return lax.rem(group + d, outer) * inner + place

    def at(plane, row_tile):
        return {"tm": plane, "tile": row_tile}

    partners = [(plane_at(d), tile) for d in range(1, planes)]
    partners += [(me, above), (me, below)]
    partners += [(me, inner_at(d)) for d in range(1, inner)]
    partners += [(me, outer_at(d)) for d in range(1, outer)]
    barrier = pltpu.get_barrier_semaphore()
    for plane, row_tile in partners:
        pl.semaphore_signal(barrier, inc=1, device_id=at(plane, row_tile), device_id_type=MESH)

    def lane(offset):
        return pl.multiple_of(lax.rem(offset + total_cols, total_cols), LANES)

    first = me * cols
    pieces = [
        (lane(first - LANES), LANES, 0),
        (lane(first), cols, LANES),
        (lane(first + cols), LANES, LANES + cols),
    ]

    def own_parts(row):
        parts = []
        for start, size, to in pieces:
            for i, ref in enumerate((cap, crow, ccol)):
                parts.append((ref.at[:, pl.ds(start, size)],
                              ext.at[i, pl.ds(row, rows), pl.ds(to, size)]))
            parts.append((term.at[:, :, pl.ds(start, size)],
                          field.at[0, :, pl.ds(row, rows), pl.ds(to, size)]))
        return parts

    def head_parts(target, source):
        begin = lane(target * cols)
        after = lane(target * cols + cols)
        return [
            (heads.at[0, :, :, pl.ds(begin, cols)], head.at[source, :, :, pl.ds(0, cols)]),
            (heads.at[0, pl.ds(1, 2), :, pl.ds(after, LANES)],
             head.at[source, pl.ds(1, 2), :, pl.ds(cols, LANES)]),
        ]

    def obs_parts(source):
        return [(ocell.at[0], cells.at[source]), (oweight.at[0], weights.at[source])]

    local = []
    for src, dst in own_parts(rows) + head_parts(me, me) + obs_parts(me):
        copy = pltpu.make_async_copy(src, dst, loc_sem.at[len(local)])
        copy.start()
        local.append(copy)
    pl.semaphore_wait(barrier, len(partners))

    def remote(src, dst, send, recv, plane, row_tile):
        return pltpu.make_async_remote_copy(
            src_ref=src, dst_ref=dst, send_sem=send, recv_sem=recv,
            device_id=at(plane, row_tile), device_id_type=MESH)

    def obs_copies(d, source):
        return [remote(src, dst, obs_send.at[d, i], obs_recv.at[d, i], plane_at(d), tile)
                for i, (src, dst) in enumerate(obs_parts(source))]

    def head_copies(d, source):
        return [remote(src, dst, head_send.at[d, i], head_recv.at[d, i], plane_at(d), tile)
                for i, (src, dst) in enumerate(head_parts(plane_at(d), source))]

    sent = []
    for d in range(1, planes):
        sent += obs_copies(d, me)
    halos = []
    for way, (row, target) in enumerate(((2 * rows, above), (0, below))):
        for i, (src, dst) in enumerate(own_parts(row)):
            halos.append(remote(src, dst, halo_send.at[way, i], halo_recv.at[way, i], me, target))
    order = sorted(range(1, planes), key=lambda d: -min(d, planes - d))
    for copy in sent + halos:
        copy.start()
    sent_heads = []
    for d in order:
        sent_heads += head_copies(d, me)
    for copy in sent_heads:
        copy.start()

    for copy in local:
        copy.wait()
    for d in range(1, planes):
        for copy in obs_copies(d, plane_at(planes - d)):
            copy.wait_recv()

    row_ids = lax.broadcasted_iota(jnp.int32, (tall, 1), 0)
    col_ids = lax.broadcasted_iota(jnp.int32, (wide, 1), 0)

    def forcing(section, carry):
        for step in range(STEPS):
            cell = cells[section, step : step + 1, :]
            cell_row = cell // total_cols
            cell_col = cell - cell_row * total_cols
            near_row = lax.rem(cell_row - tile * rows + rows + total_rows, total_rows)
            near_col = lax.rem(cell_col - me * cols + LANES + total_cols, total_cols)
            row_hit = near_row == row_ids
            col_hit = jnp.where(near_col == col_ids, 1.0, 0.0).astype(jnp.bfloat16)
            parts = []
            for member in range(2):
                rest = weights[section, step, member : member + 1, :]
                for _ in range(3):
                    part = rest.astype(jnp.bfloat16).astype(jnp.float32)
                    rest = rest - part
                    parts.append(jnp.where(row_hit, part, 0.0).astype(jnp.bfloat16))
            stacked = jnp.concatenate(parts, axis=0)
            got = lax.dot_general(stacked, col_hit, (((1,), (1,)), ((), ())),
                                  preferred_element_type=jnp.float32)
            for member in range(2):
                begin = 3 * member * tall
                force[section, step, member] = (
                    got[begin : begin + tall]
                    + got[begin + tall : begin + 2 * tall]
                    + got[begin + 2 * tall : begin + 3 * tall])
        return carry

    half = planes // 2
    lax.fori_loop(half, planes, forcing, 0)

    for copy in halos:
        copy.wait_recv()

    def activity(shift, j):
        row_tile = lax.rem(tile + shift + tiles, tiles)
        block = lax.rem(first - LANES + j * LANES + total_cols, total_cols) // block_cols
        return mask[(row_tile * rows) // block_rows, block].astype(jnp.float32)

    lane_id = lax.broadcasted_iota(jnp.int32, (rows, LANES), 1)
    row_id = lax.broadcasted_iota(jnp.int32, (rows, LANES), 0)
    act_bands, pair_bands, down_bands = [], [], []
    for band in range(3):
        act_row, pair_row, down_row = [], [], []
        last_row = lax.rem(tile + band - 1 + tiles, tiles) == tiles - 1
        for j in range(wide // LANES):
            here = activity(band - 1, j)
            last_col = lax.rem(first + j * LANES + total_cols, total_cols) == 0
            beside = jnp.where(last_col, 0.0, activity(band - 1, j + 1))
            under = jnp.where(last_row, 0.0, activity(band, j))
            act_row.append(jnp.full((rows, LANES), here, jnp.float32))
            pair_row.append(here * jnp.where(lane_id == LANES - 1, beside, here))
            down_row.append(here * jnp.where(row_id == rows - 1, under, here))
        act_bands.append(jnp.concatenate(act_row, axis=1))
        pair_bands.append(jnp.concatenate(pair_row, axis=1))
        down_bands.append(jnp.concatenate(down_row, axis=1))
    pair_core = pair_bands[1][:, LANES : LANES + cols]
    active = jnp.concatenate(act_bands, axis=0)
    east = ext[1] * jnp.concatenate(pair_bands, axis=0)
    south = ext[2] * jnp.concatenate(down_bands, axis=0)
    west = pltpu.roll(east, 1, 1)
    north = pltpu.roll(south, 1, 0)
    capacity = ext[0]
    inverse = 1.0 / (capacity + east + west + south + north)
    coef[0] = east * inverse
    coef[1] = west * inverse
    coef[2] = south * inverse
    coef[3] = north * inverse
    coef[4] = active * capacity * inverse
    coef[5] = active * inverse

    sub_id = lax.broadcasted_iota(jnp.int32, (1, 8, wide), 1)
    strips = tall // 8

    def stencil(source, i):
        start = pl.multiple_of(i * 8, 8)
        before = pl.multiple_of(jnp.maximum(i - 1, 0) * 8, 8)
        after = pl.multiple_of(jnp.minimum(i + 1, strips - 1) * 8, 8)
        here = source[:, pl.ds(start, 8), :]
        up = jnp.where(sub_id == 0, pltpu.roll(source[:, pl.ds(before, 8), :], 1, 1),
                       pltpu.roll(here, 1, 1))
        down = jnp.where(sub_id == 7, pltpu.roll(source[:, pl.ds(after, 8), :], 7, 1),
                         pltpu.roll(here, 7, 1))
        right = pltpu.roll(here, wide - 1, 2)
        left = pltpu.roll(here, 1, 2)
        strip = pl.ds(start, 8)
        total = (coef[0, strip, :][None] * right + coef[1, strip, :][None] * left
                 + coef[2, strip, :][None] * down + coef[3, strip, :][None] * up)
        return here, total, strip

    def one_step(now, section, step, skip):
        def first_sweep(i, carry):
            here, total, strip = stencil(now, i)
            part = (coef[4, strip, :][None] * here
                    + coef[5, strip, :][None] * force[section, step, :, strip, :])
            rhs[:, strip, :] = part
            mid[:, strip, :] = part + total
            return carry

        def second_sweep(i, carry):
            _, total, strip = stencil(mid, i)
            now[:, strip, :] = rhs[:, strip, :] + total
            return carry

        lax.fori_loop(skip, strips - skip, first_sweep, 0)
        lax.fori_loop(skip, strips - skip, second_sweep, 0)
        saved[section, step] = now[:, rows : 2 * rows, LANES:]

    def start_copy(section, d):
        return remote(saved.at[section, 0, :, :, pl.ds(0, cols)],
                      out_a.at[0, :, :, pl.ds(pl.multiple_of(first, LANES), cols)],
                      start_send.at[d], start_recv.at[d], section, tile)

    def own_start():
        return pltpu.make_async_copy(
            saved.at[me, 0, :, :, pl.ds(0, cols)],
            out_a.at[0, :, :, pl.ds(pl.multiple_of(first, LANES), cols)],
            loc_sem.at[0])

    mids = []
    for phase in range(2):
        now = field.at[phase]

        def one_section(turn, carry):
            section = planes - 1 - phase * half - turn
            skip = turn * 2 * STEPS // 8
            for step in reversed(range(STEPS)):
                one_step(now, section, step, skip)
            d = lax.rem(section - me + planes, planes)

            @pl.when(section != me)
            def _():
                start_copy(section, d).start()

            @pl.when(section == me)
            def _():
                own_start().start()

            return carry

        lax.fori_loop(0, half, one_section, 0)
        if phase == 0:
            core = pl.ds(rows, rows)
            field[1, :, rows : 2 * rows, :] = field[0, :, rows : 2 * rows, :]
            for way, (row, target) in enumerate(((2 * rows, above), (0, below))):
                copy = remote(field.at[0, :, core, :], field.at[1, :, pl.ds(row, rows), :],
                              mid_send.at[way], mid_recv.at[way], me, target)
                copy.start()
                mids.append(copy)
            lax.fori_loop(0, half, forcing, 0)
            for copy in mids:
                copy.wait_recv()


    def sums(turn, carry):
        sens, store_0, store_1 = carry
        d = jnp.where(turn % 2 == 1, (turn + 1) // 2, lax.rem(planes - turn // 2, planes))
        section = plane_at(planes - d)

        @pl.when(turn > 0)
        def _():
            for copy in head_copies(d, section):
                copy.wait_recv()

        for step in range(STEPS):
            a_0 = saved[section, step, 0]
            a_1 = saved[section, step, 1]
            later = head[section, step + 1]
            both = a_0 + a_1
            jump = ((pltpu.roll(both, edge - 1, 1) - both)
                    * (pltpu.roll(later, edge - 1, 1) - later))
            sens = sens + jump[:, :cols]
            change = later[:, :cols] - head[section, step, :, pl.ds(0, cols)]
            store_0 = store_0 + a_0[:, :cols] * change
            store_1 = store_1 + a_1[:, :cols] * change
        return sens, store_0, store_1

    zero = jnp.zeros((rows, cols), jnp.float32)
    sens, store_0, store_1 = lax.fori_loop(0, planes, sums, (zero, zero, zero))
    out_c[...] = sens * pair_core
    cap_core = ext[0, rows : 2 * rows, LANES : LANES + cols]
    tile_lane = lax.broadcasted_iota(jnp.int32, (8, LANES), 1)
    part = jnp.where(tile_lane == 0, jnp.sum(store_0 * cap_core), 0.0)
    part = jnp.where(tile_lane == 1, jnp.sum(store_1 * cap_core), part)

    reduce_sends = []

    def exchange(value, slots, place_here, count, partner, base):
        slots[place_here] = value
        copies = []
        for d in range(1, count):
            plane, row_tile = partner(d)
            copies.append(remote(slots.at[place_here], slots.at[place_here],
                                 red_send.at[base + d], red_recv.at[base + d], plane, row_tile))
        for copy in copies:
            copy.start()
        for d in range(1, count):
            source = lax.rem(place_here + count - d, count)
            plane, row_tile = partner(d)
            remote(slots.at[source], slots.at[source], red_send.at[base + d],
                   red_recv.at[base + d], plane, row_tile).wait_recv()
        reduce_sends.extend(copies)
        total = slots[0]
        for i in range(1, count):
            total = total + slots[i]
        return total

    part = exchange(part, red_b, place, inner, lambda d: (me, inner_at(d)), 0)
    part = exchange(part, red_c, group, outer, lambda d: (me, outer_at(d)), inner)
    part = exchange(part, red_a, me, planes, lambda d: (plane_at(d), tile), inner + outer)
    out_s[0] = jnp.sum(jnp.where(tile_lane[:1] == 0, part[:1], 0.0))
    out_s[1] = jnp.sum(jnp.where(tile_lane[:1] == 1, part[:1], 0.0))

    own_start().wait()
    for d in range(1, planes):
        source = plane_at(planes - d)
        remote(saved.at[me, 0, :, :, pl.ds(0, cols)],
               out_a.at[0, :, :, pl.ds(pl.multiple_of(source * cols, LANES), cols)],
               start_send.at[d], start_recv.at[d], plane_at(d), tile).wait_recv()
    for d in range(1, planes):
        start_copy(plane_at(d), d).wait_send()
    for copy in sent + halos + sent_heads + mids + reduce_sends:
        copy.wait_send()


def solution(mesh):
    planes, tiles = mesh.shape["tm"], mesh.shape["tile"]
    inner = min(8, tiles // 2)
    outer = tiles // inner

    def shards(heads, capacity, cond_row, cond_col, terminal, obs_cell, obs_weight, block_mask):
        rows, total_cols = capacity.shape
        cols = total_cols // planes
        wide, tall, edge = cols + 2 * LANES, 3 * rows, cols + LANES
        observed = obs_cell.shape[2]
        block_rows = rows * tiles // block_mask.shape[0]
        block_cols = total_cols // block_mask.shape[1]
        cfg = (planes, tiles, inner, rows, cols, total_cols, block_rows, block_cols)
        f32 = jnp.float32
        dma = pltpu.SemaphoreType.DMA
        any_spec = pl.BlockSpec(memory_space=pl.ANY)
        out = pl.pallas_call(
            functools.partial(kernel, cfg),
            out_shape=(
                jax.ShapeDtypeStruct((1, 2, rows, total_cols), f32),
                jax.ShapeDtypeStruct((rows, cols), f32),
                jax.ShapeDtypeStruct((2,), f32),
            ),
            in_specs=[any_spec] * 7 + [pl.BlockSpec(memory_space=pltpu.SMEM)],
            out_specs=(any_spec, pl.BlockSpec(memory_space=pltpu.VMEM),
                       pl.BlockSpec(memory_space=pltpu.SMEM)),
            scratch_shapes=[
                pltpu.VMEM((3, tall, wide), f32),
                pltpu.VMEM((2, 2, tall, wide), f32),
                pltpu.VMEM((2, tall, wide), f32),
                pltpu.VMEM((2, tall, wide), f32),
                pltpu.VMEM((6, tall, wide), f32),
                pltpu.VMEM((planes, STEPS, 2, tall, wide), f32),
                pltpu.VMEM((planes, STEPS, observed), jnp.int32),
                pltpu.VMEM((planes, STEPS, 2, observed), f32),
                pltpu.VMEM((planes, 3, rows, edge), f32),
                pltpu.VMEM((planes, STEPS, 2, rows, edge), f32),
                pltpu.VMEM((planes, 8, LANES), f32),
                pltpu.VMEM((inner, 8, LANES), f32),
                pltpu.VMEM((outer, 8, LANES), f32),
                dma((16,)),
                dma((2, 12)),
                dma((2, 12)),
                dma((planes, 2)),
                dma((planes, 2)),
                dma((planes, 2)),
                dma((planes, 2)),
                dma((2,)),
                dma((2,)),
                dma((planes,)),
                dma((planes,)),
                dma((planes + inner + outer,)),
                dma((planes + inner + outer,)),
            ],
            compiler_params=pltpu.CompilerParams(
                collective_id=0, has_side_effects=True, vmem_limit_bytes=67043328
            ),
        )(heads, capacity, cond_row, cond_col, terminal, obs_cell, obs_weight, block_mask)
        return out

    in_specs = (
        P("tm", None, "tile", None),
        P("tile", None),
        P("tile", None),
        P("tile", None),
        P(None, "tile", None),
        P("tm", None, None),
        P("tm", None, None, None),
        P(),
    )
    out_specs = (P("tm", None, "tile", None), P("tile", "tm"), P())
    return jax.shard_map(
        shards, mesh=mesh, in_specs=in_specs, out_specs=out_specs, check_vma=False
    )
```

```python
import functools

import jax
import jax.numpy as jnp
from jax import lax
from jax.experimental import pallas as pl
from jax.experimental.pallas import tpu as pltpu
from jax.sharding import PartitionSpec as P

STEPS = 2
LANES = 128
MESH = pl.DeviceIdType.MESH


def kernel(cfg, heads, cap, crow, ccol, term, ocell, oweight, mask, out_a, out_c, out_s,
           ext, field, mid, rhs, coef, force, cells, weights, head, saved, red_a, red_b,
           loc_sem, halo_send, halo_recv, obs_send, obs_recv, head_send, head_recv,
           mid_send, mid_recv, start_send, start_recv, red_send, red_recv):
    planes, tiles, rows, cols, total_cols, block_rows, block_cols = cfg
    wide = cols + 2 * LANES
    tall = 3 * rows
    edge = cols + LANES
    total_rows = rows * tiles
    me = lax.axis_index("tm")
    tile = lax.axis_index("tile")
    above = lax.rem(tile + tiles - 1, tiles)
    below = lax.rem(tile + 1, tiles)

    def plane_at(d):
        return lax.rem(me + d, planes)

    def tile_at(d):
        return lax.rem(tile + d, tiles)

    def at(plane, row_tile):
        return {"tm": plane, "tile": row_tile}

    partners = [(plane_at(d), tile) for d in range(1, planes)]
    partners += [(me, tile_at(d)) for d in range(1, tiles)]
    barrier = pltpu.get_barrier_semaphore()
    for plane, row_tile in partners:
        pl.semaphore_signal(barrier, inc=1, device_id=at(plane, row_tile), device_id_type=MESH)

    def lane(offset):
        return pl.multiple_of(lax.rem(offset + total_cols, total_cols), LANES)

    first = me * cols
    pieces = [
        (lane(first - LANES), LANES, 0),
        (lane(first), cols, LANES),
        (lane(first + cols), LANES, LANES + cols),
    ]

    def own_parts(row):
        parts = []
        for start, size, to in pieces:
            for i, ref in enumerate((cap, crow, ccol)):
                parts.append((ref.at[:, pl.ds(start, size)],
                              ext.at[i, pl.ds(row, rows), pl.ds(to, size)]))
            parts.append((term.at[:, :, pl.ds(start, size)],
                          field.at[0, :, pl.ds(row, rows), pl.ds(to, size)]))
        return parts

    def head_parts(target, source):
        begin = lane(target * cols)
        after = lane(target * cols + cols)
        return [
            (heads.at[0, :, :, pl.ds(begin, cols)], head.at[source, :, :, pl.ds(0, cols)]),
            (heads.at[0, pl.ds(1, 2), :, pl.ds(after, LANES)],
             head.at[source, pl.ds(1, 2), :, pl.ds(cols, LANES)]),
        ]

    def obs_parts(source):
        return [(ocell.at[0], cells.at[source]), (oweight.at[0], weights.at[source])]

    local = []
    for src, dst in own_parts(rows) + head_parts(me, me) + obs_parts(me):
        copy = pltpu.make_async_copy(src, dst, loc_sem.at[len(local)])
        copy.start()
        local.append(copy)
    pl.semaphore_wait(barrier, len(partners))

    def remote(src, dst, send, recv, plane, row_tile):
        return pltpu.make_async_remote_copy(
            src_ref=src, dst_ref=dst, send_sem=send, recv_sem=recv,
            device_id=at(plane, row_tile), device_id_type=MESH)

    def obs_copies(d, source):
        return [remote(src, dst, obs_send.at[d, i], obs_recv.at[d, i], plane_at(d), tile)
                for i, (src, dst) in enumerate(obs_parts(source))]

    def head_copies(d, source):
        return [remote(src, dst, head_send.at[d, i], head_recv.at[d, i], plane_at(d), tile)
                for i, (src, dst) in enumerate(head_parts(plane_at(d), source))]

    sent = []
    for d in range(1, planes):
        sent += obs_copies(d, me)
    halos = []
    for way, (row, target) in enumerate(((2 * rows, above), (0, below))):
        for i, (src, dst) in enumerate(own_parts(row)):
            halos.append(remote(src, dst, halo_send.at[way, i], halo_recv.at[way, i], me, target))
    order = sorted(range(1, planes), key=lambda d: -min(d, planes - d))
    for copy in sent + halos:
        copy.start()
    sent_heads = []
    for d in order:
        sent_heads += head_copies(d, me)
    for copy in sent_heads:
        copy.start()

    for copy in local:
        copy.wait()
    for d in range(1, planes):
        for copy in obs_copies(d, plane_at(planes - d)):
            copy.wait_recv()

    row_ids = lax.broadcasted_iota(jnp.int32, (tall, 1), 0)
    col_ids = lax.broadcasted_iota(jnp.int32, (wide, 1), 0)

    def forcing(section, carry):
        for step in range(STEPS):
            cell = cells[section, step : step + 1, :]
            cell_row = cell // total_cols
            cell_col = cell - cell_row * total_cols
            near_row = lax.rem(cell_row - tile * rows + rows + total_rows, total_rows)
            near_col = lax.rem(cell_col - me * cols + LANES + total_cols, total_cols)
            row_hit = near_row == row_ids
            col_hit = jnp.where(near_col == col_ids, 1.0, 0.0).astype(jnp.bfloat16)
            parts = []
            for member in range(2):
                rest = weights[section, step, member : member + 1, :]
                for _ in range(3):
                    part = rest.astype(jnp.bfloat16).astype(jnp.float32)
                    rest = rest - part
                    parts.append(jnp.where(row_hit, part, 0.0).astype(jnp.bfloat16))
            stacked = jnp.concatenate(parts, axis=0)
            got = lax.dot_general(stacked, col_hit, (((1,), (1,)), ((), ())),
                                  preferred_element_type=jnp.float32)
            for member in range(2):
                begin = 3 * member * tall
                force[section, step, member] = (
                    got[begin : begin + tall]
                    + got[begin + tall : begin + 2 * tall]
                    + got[begin + 2 * tall : begin + 3 * tall])
        return carry

    half = planes // 2
    lax.fori_loop(half, planes, forcing, 0)

    for copy in halos:
        copy.wait_recv()

    def activity(shift, j):
        row_tile = lax.rem(tile + shift + tiles, tiles)
        block = lax.rem(first - LANES + j * LANES + total_cols, total_cols) // block_cols
        return mask[(row_tile * rows) // block_rows, block].astype(jnp.float32)

    lane_id = lax.broadcasted_iota(jnp.int32, (rows, LANES), 1)
    row_id = lax.broadcasted_iota(jnp.int32, (rows, LANES), 0)
    act_bands, pair_bands, down_bands = [], [], []
    for band in range(3):
        act_row, pair_row, down_row = [], [], []
        last_row = lax.rem(tile + band - 1 + tiles, tiles) == tiles - 1
        for j in range(wide // LANES):
            here = activity(band - 1, j)
            last_col = lax.rem(first + j * LANES + total_cols, total_cols) == 0
            beside = jnp.where(last_col, 0.0, activity(band - 1, j + 1))
            under = jnp.where(last_row, 0.0, activity(band, j))
            act_row.append(jnp.full((rows, LANES), here, jnp.float32))
            pair_row.append(here * jnp.where(lane_id == LANES - 1, beside, here))
            down_row.append(here * jnp.where(row_id == rows - 1, under, here))
        act_bands.append(jnp.concatenate(act_row, axis=1))
        pair_bands.append(jnp.concatenate(pair_row, axis=1))
        down_bands.append(jnp.concatenate(down_row, axis=1))
    pair_core = pair_bands[1][:, LANES : LANES + cols]
    active = jnp.concatenate(act_bands, axis=0)
    east = ext[1] * jnp.concatenate(pair_bands, axis=0)
    south = ext[2] * jnp.concatenate(down_bands, axis=0)
    west = pltpu.roll(east, 1, 1)
    north = pltpu.roll(south, 1, 0)
    capacity = ext[0]
    inverse = 1.0 / (capacity + east + west + south + north)
    coef[0] = east * inverse
    coef[1] = west * inverse
    coef[2] = south * inverse
    coef[3] = north * inverse
    coef[4] = active * capacity * inverse
    coef[5] = active * inverse

    sub_id = lax.broadcasted_iota(jnp.int32, (1, 8, wide), 1)
    strips = tall // 8

    def stencil(source, i):
        start = pl.multiple_of(i * 8, 8)
        before = pl.multiple_of(jnp.maximum(i - 1, 0) * 8, 8)
        after = pl.multiple_of(jnp.minimum(i + 1, strips - 1) * 8, 8)
        here = source[:, pl.ds(start, 8), :]
        up = jnp.where(sub_id == 0, pltpu.roll(source[:, pl.ds(before, 8), :], 1, 1),
                       pltpu.roll(here, 1, 1))
        down = jnp.where(sub_id == 7, pltpu.roll(source[:, pl.ds(after, 8), :], 7, 1),
                         pltpu.roll(here, 7, 1))
        right = pltpu.roll(here, wide - 1, 2)
        left = pltpu.roll(here, 1, 2)
        strip = pl.ds(start, 8)
        total = (coef[0, strip, :][None] * right + coef[1, strip, :][None] * left
                 + coef[2, strip, :][None] * down + coef[3, strip, :][None] * up)
        return here, total, strip

    def one_step(now, section, step, skip):
        def first_sweep(i, carry):
            here, total, strip = stencil(now, i)
            part = (coef[4, strip, :][None] * here
                    + coef[5, strip, :][None] * force[section, step, :, strip, :])
            rhs[:, strip, :] = part
            mid[:, strip, :] = part + total
            return carry

        def second_sweep(i, carry):
            _, total, strip = stencil(mid, i)
            now[:, strip, :] = rhs[:, strip, :] + total
            return carry

        lax.fori_loop(skip, strips - skip, first_sweep, 0, unroll=True)
        lax.fori_loop(skip, strips - skip, second_sweep, 0, unroll=True)
        saved[section, step] = now[:, rows : 2 * rows, LANES:]

    def start_copy(section, d):
        return remote(saved.at[section, 0, :, :, pl.ds(0, cols)],
                      out_a.at[0, :, :, pl.ds(pl.multiple_of(first, LANES), cols)],
                      start_send.at[d], start_recv.at[d], section, tile)

    def own_start():
        return pltpu.make_async_copy(
            saved.at[me, 0, :, :, pl.ds(0, cols)],
            out_a.at[0, :, :, pl.ds(pl.multiple_of(first, LANES), cols)],
            loc_sem.at[0])

    mids = []
    for phase in range(2):
        now = field.at[phase]

        def one_section(skip, turn, carry):
            section = planes - 1 - phase * half - turn
            for step in reversed(range(STEPS)):
                one_step(now, section, step, skip)
            d = lax.rem(section - me + planes, planes)

            @pl.when(section != me)
            def _():
                start_copy(section, d).start()

            @pl.when(section == me)
            def _():
                own_start().start()

            return carry

        lax.fori_loop(0, half // 2, functools.partial(one_section, 0), 0)
        lax.fori_loop(half // 2, half, functools.partial(one_section, 1), 0)
        if phase == 0:
            core = pl.ds(rows, rows)
            field[1, :, rows : 2 * rows, :] = field[0, :, rows : 2 * rows, :]
            for way, (row, target) in enumerate(((2 * rows, above), (0, below))):
                copy = remote(field.at[0, :, core, :], field.at[1, :, pl.ds(row, rows), :],
                              mid_send.at[way], mid_recv.at[way], me, target)
                copy.start()
                mids.append(copy)
            lax.fori_loop(0, half, forcing, 0)
            for copy in mids:
                copy.wait_recv()


    def sums(turn, carry):
        sens, store_0, store_1 = carry
        d = jnp.where(turn % 2 == 1, (turn + 1) // 2, lax.rem(planes - turn // 2, planes))
        section = plane_at(planes - d)

        @pl.when(turn > 0)
        def _():
            for copy in head_copies(d, section):
                copy.wait_recv()

        for step in range(STEPS):
            a_0 = saved[section, step, 0]
            a_1 = saved[section, step, 1]
            later = head[section, step + 1]
            both = a_0 + a_1
            jump = ((pltpu.roll(both, edge - 1, 1) - both)
                    * (pltpu.roll(later, edge - 1, 1) - later))
            sens = sens + jump[:, :cols]
            change = later[:, :cols] - head[section, step, :, pl.ds(0, cols)]
            store_0 = store_0 + a_0[:, :cols] * change
            store_1 = store_1 + a_1[:, :cols] * change
        return sens, store_0, store_1

    zero = jnp.zeros((rows, cols), jnp.float32)
    sens, store_0, store_1 = lax.fori_loop(0, planes, sums, (zero, zero, zero))
    out_c[...] = sens * pair_core
    cap_core = ext[0, rows : 2 * rows, LANES : LANES + cols]
    tile_lane = lax.broadcasted_iota(jnp.int32, (1, LANES), 1)
    part = jnp.where(tile_lane == 0, jnp.sum(store_0 * cap_core), 0.0)
    part = jnp.where(tile_lane == 1, jnp.sum(store_1 * cap_core), part)

    reduce_sends = []

    def exchange(value, slots, place_here, count, partner, base):
        slots[place_here] = value
        copies = []
        for d in range(1, count):
            plane, row_tile = partner(d)
            copies.append(remote(slots.at[place_here], slots.at[place_here],
                                 red_send.at[base + d], red_recv.at[base + d], plane, row_tile))
        for copy in copies:
            copy.start()
        for d in range(1, count):
            source = lax.rem(place_here + count - d, count)
            plane, row_tile = partner(d)
            remote(slots.at[source], slots.at[source], red_send.at[base + d],
                   red_recv.at[base + d], plane, row_tile).wait_recv()
        reduce_sends.extend(copies)
        return jnp.sum(slots[...], axis=0)

    part = exchange(part, red_b, tile, tiles, lambda d: (me, tile_at(d)), 0)
    part = exchange(part, red_a, me, planes, lambda d: (plane_at(d), tile), tiles)
    out_s[0] = jnp.sum(jnp.where(tile_lane == 0, part, 0.0))
    out_s[1] = jnp.sum(jnp.where(tile_lane == 1, part, 0.0))

    own_start().wait()
    for d in range(1, planes):
        source = plane_at(planes - d)
        remote(saved.at[me, 0, :, :, pl.ds(0, cols)],
               out_a.at[0, :, :, pl.ds(pl.multiple_of(source * cols, LANES), cols)],
               start_send.at[d], start_recv.at[d], plane_at(d), tile).wait_recv()
    for d in range(1, planes):
        start_copy(plane_at(d), d).wait_send()
    for copy in sent + halos + sent_heads + mids + reduce_sends:
        copy.wait_send()


def solution(mesh):
    planes, tiles = mesh.shape["tm"], mesh.shape["tile"]

    def shards(heads, capacity, cond_row, cond_col, terminal, obs_cell, obs_weight, block_mask):
        rows, total_cols = capacity.shape
        cols = total_cols // planes
        wide, tall, edge = cols + 2 * LANES, 3 * rows, cols + LANES
        observed = obs_cell.shape[2]
        block_rows = rows * tiles // block_mask.shape[0]
        block_cols = total_cols // block_mask.shape[1]
        cfg = (planes, tiles, rows, cols, total_cols, block_rows, block_cols)
        f32 = jnp.float32
        dma = pltpu.SemaphoreType.DMA
        any_spec = pl.BlockSpec(memory_space=pl.ANY)
        out = pl.pallas_call(
            functools.partial(kernel, cfg),
            out_shape=(
                jax.ShapeDtypeStruct((1, 2, rows, total_cols), f32),
                jax.ShapeDtypeStruct((rows, cols), f32),
                jax.ShapeDtypeStruct((2,), f32),
            ),
            in_specs=[any_spec] * 7 + [pl.BlockSpec(memory_space=pltpu.SMEM)],
            out_specs=(any_spec, pl.BlockSpec(memory_space=pltpu.VMEM),
                       pl.BlockSpec(memory_space=pltpu.SMEM)),
            scratch_shapes=[
                pltpu.VMEM((3, tall, wide), f32),
                pltpu.VMEM((2, 2, tall, wide), f32),
                pltpu.VMEM((2, tall, wide), f32),
                pltpu.VMEM((2, tall, wide), f32),
                pltpu.VMEM((6, tall, wide), f32),
                pltpu.VMEM((planes, STEPS, 2, tall, wide), f32),
                pltpu.VMEM((planes, STEPS, observed), jnp.int32),
                pltpu.VMEM((planes, STEPS, 2, observed), f32),
                pltpu.VMEM((planes, 3, rows, edge), f32),
                pltpu.VMEM((planes, STEPS, 2, rows, edge), f32),
                pltpu.VMEM((planes, 1, LANES), f32),
                pltpu.VMEM((tiles, 1, LANES), f32),
                dma((16,)),
                dma((2, 12)),
                dma((2, 12)),
                dma((planes, 2)),
                dma((planes, 2)),
                dma((planes, 2)),
                dma((planes, 2)),
                dma((2,)),
                dma((2,)),
                dma((planes,)),
                dma((planes,)),
                dma((planes + tiles,)),
                dma((planes + tiles,)),
            ],
            compiler_params=pltpu.CompilerParams(
                collective_id=0, has_side_effects=True, vmem_limit_bytes=67043328
            ),
        )(heads, capacity, cond_row, cond_col, terminal, obs_cell, obs_weight, block_mask)
        return out

    in_specs = (
        P("tm", None, "tile", None),
        P("tile", None),
        P("tile", None),
        P("tile", None),
        P(None, "tile", None),
        P("tm", None, None),
        P("tm", None, None, None),
        P(),
    )
    out_specs = (P("tm", None, "tile", None), P("tile", "tm"), P())
    return jax.shard_map(
        shards, mesh=mesh, in_specs=in_specs, out_specs=out_specs, check_vma=False
    )
```

```python
import functools

import jax
import jax.numpy as jnp
from jax import lax
from jax.experimental import pallas as pl
from jax.experimental.pallas import tpu as pltpu
from jax.sharding import PartitionSpec as P

STEPS = 2
LANES = 128
MESH = pl.DeviceIdType.MESH


def kernel(cfg, heads, cap, crow, ccol, term, ocell, oweight, mask, out_a, out_c, out_s,
           ext, field, mid, rhs, coef, force, cells, weights, head, saved, red_a, red_b, edge_out, edge_in,
           loc_sem, halo_send, halo_recv, obs_send, obs_recv, head_send, head_recv,
           mid_send, mid_recv, start_send, start_recv, red_send, red_recv,
           edge_send, edge_recv):
    planes, tiles, rows, cols, total_cols, block_rows, block_cols = cfg
    wide = cols + 2 * LANES
    tall = 3 * rows
    edge = cols + LANES
    total_rows = rows * tiles
    me = lax.axis_index("tm")
    tile = lax.axis_index("tile")
    above = lax.rem(tile + tiles - 1, tiles)
    below = lax.rem(tile + 1, tiles)

    def plane_at(d):
        return lax.rem(me + d, planes)

    def tile_at(d):
        return lax.rem(tile + d, tiles)

    def at(plane, row_tile):
        return {"tm": plane, "tile": row_tile}

    partners = [(plane_at(d), tile) for d in range(1, planes)]
    partners += [(me, tile_at(d)) for d in range(1, tiles)]
    barrier = pltpu.get_barrier_semaphore()
    for plane, row_tile in partners:
        pl.semaphore_signal(barrier, inc=1, device_id=at(plane, row_tile), device_id_type=MESH)

    def lane(offset):
        return pl.multiple_of(lax.rem(offset + total_cols, total_cols), LANES)

    first = me * cols
    pieces = [
        (lane(first - LANES), LANES, 0),
        (lane(first), cols, LANES),
        (lane(first + cols), LANES, LANES + cols),
    ]

    def own_parts(row):
        parts = []
        for start, size, to in pieces:
            for i, ref in enumerate((cap, crow, ccol)):
                parts.append((ref.at[:, pl.ds(start, size)],
                              ext.at[i, pl.ds(row, rows), pl.ds(to, size)]))
            parts.append((term.at[:, :, pl.ds(start, size)],
                          field.at[0, :, pl.ds(row, rows), pl.ds(to, size)]))
        return parts

    def head_parts(target, source):
        begin = lane(target * cols)
        return [(heads.at[0, :, :, pl.ds(begin, cols)], head.at[source])]

    def obs_parts(source):
        return [(ocell.at[0], cells.at[source]), (oweight.at[0], weights.at[source])]

    local = []
    for src, dst in own_parts(rows) + head_parts(me, me) + obs_parts(me):
        copy = pltpu.make_async_copy(src, dst, loc_sem.at[len(local)])
        copy.start()
        local.append(copy)
    pl.semaphore_wait(barrier, len(partners))

    def remote(src, dst, send, recv, plane, row_tile):
        return pltpu.make_async_remote_copy(
            src_ref=src, dst_ref=dst, send_sem=send, recv_sem=recv,
            device_id=at(plane, row_tile), device_id_type=MESH)

    def obs_copies(d, source):
        return [remote(src, dst, obs_send.at[d, i], obs_recv.at[d, i], plane_at(d), tile)
                for i, (src, dst) in enumerate(obs_parts(source))]

    def head_copies(d, source):
        return [remote(src, dst, head_send.at[d, i], head_recv.at[d, i], plane_at(d), tile)
                for i, (src, dst) in enumerate(head_parts(plane_at(d), source))]

    sent = []
    for d in range(1, planes):
        sent += obs_copies(d, me)
    halos = []
    for way, (row, target) in enumerate(((2 * rows, above), (0, below))):
        for i, (src, dst) in enumerate(own_parts(row)):
            halos.append(remote(src, dst, halo_send.at[way, i], halo_recv.at[way, i], me, target))
    order = sorted(range(1, planes), key=lambda d: -min(d, planes - d))
    for copy in sent + halos:
        copy.start()
    sent_heads = []
    for d in order:
        sent_heads += head_copies(d, me)
    for copy in sent_heads:
        copy.start()

    for copy in local:
        copy.wait()
    for d in range(1, planes):
        for copy in obs_copies(d, plane_at(planes - d)):
            copy.wait_recv()

    row_ids = lax.broadcasted_iota(jnp.int32, (tall, 1), 0)
    col_ids = lax.broadcasted_iota(jnp.int32, (wide, 1), 0)

    def forcing(section, carry):
        for step in range(STEPS):
            cell = cells[section, step : step + 1, :]
            cell_row = cell // total_cols
            cell_col = cell - cell_row * total_cols
            near_row = lax.rem(cell_row - tile * rows + rows + total_rows, total_rows)
            near_col = lax.rem(cell_col - me * cols + LANES + total_cols, total_cols)
            row_hit = near_row == row_ids
            col_hit = jnp.where(near_col == col_ids, 1.0, 0.0).astype(jnp.bfloat16)
            parts = []
            for member in range(2):
                rest = weights[section, step, member : member + 1, :]
                for _ in range(3):
                    part = rest.astype(jnp.bfloat16).astype(jnp.float32)
                    rest = rest - part
                    parts.append(jnp.where(row_hit, part, 0.0).astype(jnp.bfloat16))
            stacked = jnp.concatenate(parts, axis=0)
            got = lax.dot_general(stacked, col_hit, (((1,), (1,)), ((), ())),
                                  preferred_element_type=jnp.float32)
            for member in range(2):
                begin = 3 * member * tall
                force[section, step, member] = (
                    got[begin : begin + tall]
                    + got[begin + tall : begin + 2 * tall]
                    + got[begin + 2 * tall : begin + 3 * tall])
        return carry

    half = planes // 2
    lax.fori_loop(half, planes, forcing, 0)

    for copy in halos:
        copy.wait_recv()

    def activity(shift, j):
        row_tile = lax.rem(tile + shift + tiles, tiles)
        block = lax.rem(first - LANES + j * LANES + total_cols, total_cols) // block_cols
        return mask[(row_tile * rows) // block_rows, block].astype(jnp.float32)

    lane_id = lax.broadcasted_iota(jnp.int32, (rows, LANES), 1)
    row_id = lax.broadcasted_iota(jnp.int32, (rows, LANES), 0)
    act_bands, pair_bands, down_bands = [], [], []
    for band in range(3):
        act_row, pair_row, down_row = [], [], []
        last_row = lax.rem(tile + band - 1 + tiles, tiles) == tiles - 1
        for j in range(wide // LANES):
            here = activity(band - 1, j)
            last_col = lax.rem(first + j * LANES + total_cols, total_cols) == 0
            beside = jnp.where(last_col, 0.0, activity(band - 1, j + 1))
            under = jnp.where(last_row, 0.0, activity(band, j))
            act_row.append(jnp.full((rows, LANES), here, jnp.float32))
            pair_row.append(here * jnp.where(lane_id == LANES - 1, beside, here))
            down_row.append(here * jnp.where(row_id == rows - 1, under, here))
        act_bands.append(jnp.concatenate(act_row, axis=1))
        pair_bands.append(jnp.concatenate(pair_row, axis=1))
        down_bands.append(jnp.concatenate(down_row, axis=1))
    pair_core = pair_bands[1][:, LANES : LANES + cols]
    active = jnp.concatenate(act_bands, axis=0)
    east = ext[1] * jnp.concatenate(pair_bands, axis=0)
    south = ext[2] * jnp.concatenate(down_bands, axis=0)
    west = pltpu.roll(east, 1, 1)
    north = pltpu.roll(south, 1, 0)
    capacity = ext[0]
    inverse = 1.0 / (capacity + east + west + south + north)
    coef[0] = east * inverse
    coef[1] = west * inverse
    coef[2] = south * inverse
    coef[3] = north * inverse
    coef[4] = active * capacity * inverse
    coef[5] = active * inverse

    sub_id = lax.broadcasted_iota(jnp.int32, (1, 8, wide), 1)
    strips = tall // 8

    def stencil(source, i):
        start = pl.multiple_of(i * 8, 8)
        before = pl.multiple_of(jnp.maximum(i - 1, 0) * 8, 8)
        after = pl.multiple_of(jnp.minimum(i + 1, strips - 1) * 8, 8)
        here = source[:, pl.ds(start, 8), :]
        up = jnp.where(sub_id == 0, pltpu.roll(source[:, pl.ds(before, 8), :], 1, 1),
                       pltpu.roll(here, 1, 1))
        down = jnp.where(sub_id == 7, pltpu.roll(source[:, pl.ds(after, 8), :], 7, 1),
                         pltpu.roll(here, 7, 1))
        right = pltpu.roll(here, wide - 1, 2)
        left = pltpu.roll(here, 1, 2)
        strip = pl.ds(start, 8)
        total = (coef[0, strip, :][None] * right + coef[1, strip, :][None] * left
                 + coef[2, strip, :][None] * down + coef[3, strip, :][None] * up)
        return here, total, strip

    def one_step(now, section, step, skip):
        def first_sweep(i, carry):
            here, total, strip = stencil(now, i)
            part = (coef[4, strip, :][None] * here
                    + coef[5, strip, :][None] * force[section, step, :, strip, :])
            rhs[:, strip, :] = part
            mid[:, strip, :] = part + total
            return carry

        def second_sweep(i, carry):
            _, total, strip = stencil(mid, i)
            now[:, strip, :] = rhs[:, strip, :] + total
            return carry

        lax.fori_loop(skip, strips - skip, first_sweep, 0, unroll=True)
        lax.fori_loop(skip, strips - skip, second_sweep, 0, unroll=True)
        saved[section, step] = now[:, rows : 2 * rows, LANES:]

    def start_copy(section, d):
        return remote(saved.at[section, 0, :, :, pl.ds(0, cols)],
                      out_a.at[0, :, :, pl.ds(pl.multiple_of(first, LANES), cols)],
                      start_send.at[d], start_recv.at[d], section, tile)

    def own_start():
        return pltpu.make_async_copy(
            saved.at[me, 0, :, :, pl.ds(0, cols)],
            out_a.at[0, :, :, pl.ds(pl.multiple_of(first, LANES), cols)],
            loc_sem.at[0])

    mids = []
    for phase in range(2):
        now = field.at[phase]

        def one_section(skip, turn, carry):
            section = planes - 1 - phase * half - turn
            for step in reversed(range(STEPS)):
                one_step(now, section, step, skip)
            d = lax.rem(section - me + planes, planes)

            @pl.when(section != me)
            def _():
                start_copy(section, d).start()

            @pl.when(section == me)
            def _():
                own_start().start()

            return carry

        lax.fori_loop(0, half // 2, functools.partial(one_section, 0), 0)
        lax.fori_loop(half // 2, half, functools.partial(one_section, 1), 0)
        if phase == 0:
            core = pl.ds(rows, rows)
            field[1, :, rows : 2 * rows, :] = field[0, :, rows : 2 * rows, :]
            for way, (row, target) in enumerate(((2 * rows, above), (0, below))):
                copy = remote(field.at[0, :, core, :], field.at[1, :, pl.ds(row, rows), :],
                              mid_send.at[way], mid_recv.at[way], me, target)
                copy.start()
                mids.append(copy)
            lax.fori_loop(0, half, forcing, 0)
            for copy in mids:
                copy.wait_recv()


    def sums(turn, carry):
        sens, store_0, store_1, jumps, begins, ends = carry
        d = jnp.where(turn % 2 == 1, (turn + 1) // 2, lax.rem(planes - turn // 2, planes))
        section = plane_at(planes - d)

        @pl.when(turn > 0)
        def _():
            for copy in head_copies(d, section):
                copy.wait_recv()

        for step in range(STEPS):
            a_0 = saved[section, step, 0]
            a_1 = saved[section, step, 1]
            later = head[section, step + 1]
            both = a_0 + a_1
            jump = pltpu.roll(both, edge - 1, 1) - both
            sens = sens + jump[:, :cols] * (pltpu.roll(later, cols - 1, 1) - later)
            here = lane_id == section * STEPS + step
            jumps = jnp.where(here, jump[:, cols - 1 : cols], jumps)
            begins = jnp.where(here, later[:, 0:1], begins)
            ends = jnp.where(here, later[:, cols - 1 : cols], ends)
            change = later - head[section, step]
            store_0 = store_0 + a_0[:, :cols] * change
            store_1 = store_1 + a_1[:, :cols] * change
        return sens, store_0, store_1, jumps, begins, ends

    zero = jnp.zeros((rows, cols), jnp.float32)
    none = jnp.zeros((rows, LANES), jnp.float32)
    sens, store_0, store_1, jumps, begins, ends = lax.fori_loop(
        0, planes, sums, (zero, zero, zero, none, none, none))
    edge_out[...] = begins
    edge_copy = remote(edge_out, edge_in, edge_send, edge_recv, plane_at(planes - 1), tile)
    edge_copy.start()
    cap_core = ext[0, rows : 2 * rows, LANES : LANES + cols]
    tile_lane = lax.broadcasted_iota(jnp.int32, (1, LANES), 1)
    part = jnp.where(tile_lane == 0, jnp.sum(store_0 * cap_core), 0.0)
    part = jnp.where(tile_lane == 1, jnp.sum(store_1 * cap_core), part)

    reduce_sends = []

    def exchange(value, slots, place_here, count, partner, base):
        slots[place_here] = value
        copies = []
        for d in range(1, count):
            plane, row_tile = partner(d)
            copies.append(remote(slots.at[place_here], slots.at[place_here],
                                 red_send.at[base + d], red_recv.at[base + d], plane, row_tile))
        for copy in copies:
            copy.start()
        for d in range(1, count):
            source = lax.rem(place_here + count - d, count)
            plane, row_tile = partner(d)
            remote(slots.at[source], slots.at[source], red_send.at[base + d],
                   red_recv.at[base + d], plane, row_tile).wait_recv()
        reduce_sends.extend(copies)
        return jnp.sum(slots[...], axis=0)

    part = exchange(part, red_b, tile, tiles, lambda d: (me, tile_at(d)), 0)
    part = exchange(part, red_a, me, planes, lambda d: (plane_at(d), tile), tiles)
    out_s[0] = jnp.sum(jnp.where(tile_lane == 0, part, 0.0))
    out_s[1] = jnp.sum(jnp.where(tile_lane == 1, part, 0.0))

    edge_copy.wait_recv()
    last = jnp.sum(jumps * (edge_in[...] - ends), axis=1, keepdims=True)
    col = lax.broadcasted_iota(jnp.int32, (rows, cols), 1)
    out_c[...] = jnp.where(col == cols - 1, last, sens) * pair_core

    own_start().wait()
    for d in range(1, planes):
        source = plane_at(planes - d)
        remote(saved.at[me, 0, :, :, pl.ds(0, cols)],
               out_a.at[0, :, :, pl.ds(pl.multiple_of(source * cols, LANES), cols)],
               start_send.at[d], start_recv.at[d], plane_at(d), tile).wait_recv()
    for d in range(1, planes):
        start_copy(plane_at(d), d).wait_send()
    for copy in sent + halos + sent_heads + mids + reduce_sends + [edge_copy]:
        copy.wait_send()


def solution(mesh):
    planes, tiles = mesh.shape["tm"], mesh.shape["tile"]

    def shards(heads, capacity, cond_row, cond_col, terminal, obs_cell, obs_weight, block_mask):
        rows, total_cols = capacity.shape
        cols = total_cols // planes
        wide, tall, edge = cols + 2 * LANES, 3 * rows, cols + LANES
        observed = obs_cell.shape[2]
        block_rows = rows * tiles // block_mask.shape[0]
        block_cols = total_cols // block_mask.shape[1]
        cfg = (planes, tiles, rows, cols, total_cols, block_rows, block_cols)
        f32 = jnp.float32
        dma = pltpu.SemaphoreType.DMA
        any_spec = pl.BlockSpec(memory_space=pl.ANY)
        out = pl.pallas_call(
            functools.partial(kernel, cfg),
            out_shape=(
                jax.ShapeDtypeStruct((1, 2, rows, total_cols), f32),
                jax.ShapeDtypeStruct((rows, cols), f32),
                jax.ShapeDtypeStruct((2,), f32),
            ),
            in_specs=[any_spec] * 7 + [pl.BlockSpec(memory_space=pltpu.SMEM)],
            out_specs=(any_spec, pl.BlockSpec(memory_space=pltpu.VMEM),
                       pl.BlockSpec(memory_space=pltpu.SMEM)),
            scratch_shapes=[
                pltpu.VMEM((3, tall, wide), f32),
                pltpu.VMEM((2, 2, tall, wide), f32),
                pltpu.VMEM((2, tall, wide), f32),
                pltpu.VMEM((2, tall, wide), f32),
                pltpu.VMEM((6, tall, wide), f32),
                pltpu.VMEM((planes, STEPS, 2, tall, wide), f32),
                pltpu.VMEM((planes, STEPS, observed), jnp.int32),
                pltpu.VMEM((planes, STEPS, 2, observed), f32),
                pltpu.VMEM((planes, 3, rows, cols), f32),
                pltpu.VMEM((planes, STEPS, 2, rows, edge), f32),
                pltpu.VMEM((planes, 1, LANES), f32),
                pltpu.VMEM((tiles, 1, LANES), f32),
                pltpu.VMEM((rows, LANES), f32),
                pltpu.VMEM((rows, LANES), f32),
                dma((16,)),
                dma((2, 12)),
                dma((2, 12)),
                dma((planes, 2)),
                dma((planes, 2)),
                dma((planes, 2)),
                dma((planes, 2)),
                dma((2,)),
                dma((2,)),
                dma((planes,)),
                dma((planes,)),
                dma((planes + tiles,)),
                dma((planes + tiles,)),
                dma(()),
                dma(()),
            ],
            compiler_params=pltpu.CompilerParams(
                collective_id=0, has_side_effects=True, vmem_limit_bytes=67043328
            ),
        )(heads, capacity, cond_row, cond_col, terminal, obs_cell, obs_weight, block_mask)
        return out

    in_specs = (
        P("tm", None, "tile", None),
        P("tile", None),
        P("tile", None),
        P("tile", None),
        P(None, "tile", None),
        P("tm", None, None),
        P("tm", None, None, None),
        P(),
    )
    out_specs = (P("tm", None, "tile", None), P("tile", "tm"), P())
    return jax.shard_map(
        shards, mesh=mesh, in_specs=in_specs, out_specs=out_specs, check_vma=False
    )
```

```python
import functools

import jax
import jax.numpy as jnp
from jax import lax
from jax.experimental import pallas as pl
from jax.experimental.pallas import tpu as pltpu
from jax.sharding import PartitionSpec as P

STEPS = 2
LANES = 128
MESH = pl.DeviceIdType.MESH


def kernel(cfg, heads, cap, crow, ccol, term, ocell, oweight, mask, out_a, out_c, out_s,
           ext, field, mid, rhs, coef, force, cells, weights, head, saved, red_a, red_b, edge_out, edge_in,
           loc_sem, halo_send, halo_recv, obs_send, obs_recv, head_send, head_recv,
           mid_send, mid_recv, start_send, start_recv, red_send, red_recv,
           edge_send, edge_recv):
    planes, tiles, rows, cols, total_cols, block_rows, block_cols = cfg
    wide = cols + 2 * LANES
    tall = 3 * rows
    edge = cols + LANES
    total_rows = rows * tiles
    me = lax.axis_index("tm")
    tile = lax.axis_index("tile")
    above = lax.rem(tile + tiles - 1, tiles)
    below = lax.rem(tile + 1, tiles)

    def plane_at(d):
        return lax.rem(me + d, planes)

    def tile_at(d):
        return lax.rem(tile + d, tiles)

    def at(plane, row_tile):
        return {"tm": plane, "tile": row_tile}

    partners = [(plane_at(d), tile) for d in range(1, planes)]
    partners += [(me, tile_at(d)) for d in range(1, tiles)]
    barrier = pltpu.get_barrier_semaphore()
    for plane, row_tile in partners:
        pl.semaphore_signal(barrier, inc=1, device_id=at(plane, row_tile), device_id_type=MESH)

    def lane(offset):
        return pl.multiple_of(lax.rem(offset + total_cols, total_cols), LANES)

    first = me * cols
    pieces = [
        (lane(first - LANES), LANES, 0),
        (lane(first), cols, LANES),
        (lane(first + cols), LANES, LANES + cols),
    ]

    def own_parts(row):
        parts = []
        for start, size, to in pieces:
            for i, ref in enumerate((cap, crow, ccol)):
                parts.append((ref.at[:, pl.ds(start, size)],
                              ext.at[i, pl.ds(row, rows), pl.ds(to, size)]))
            parts.append((term.at[:, :, pl.ds(start, size)],
                          field.at[0, :, pl.ds(row, rows), pl.ds(to, size)]))
        return parts

    def head_parts(target, source):
        begin = lane(target * cols)
        return [(heads.at[0, :, :, pl.ds(begin, cols)], head.at[source])]

    def obs_parts(source):
        return [(ocell.at[0], cells.at[source]), (oweight.at[0], weights.at[source])]

    local = []
    for src, dst in own_parts(rows) + head_parts(me, me) + obs_parts(me):
        copy = pltpu.make_async_copy(src, dst, loc_sem.at[len(local)])
        copy.start()
        local.append(copy)
    pl.semaphore_wait(barrier, len(partners))

    def remote(src, dst, send, recv, plane, row_tile):
        return pltpu.make_async_remote_copy(
            src_ref=src, dst_ref=dst, send_sem=send, recv_sem=recv,
            device_id=at(plane, row_tile), device_id_type=MESH)

    def obs_copies(d, source):
        return [remote(src, dst, obs_send.at[d, i], obs_recv.at[d, i], plane_at(d), tile)
                for i, (src, dst) in enumerate(obs_parts(source))]

    def head_copies(d, source):
        return [remote(src, dst, head_send.at[d, i], head_recv.at[d, i], plane_at(d), tile)
                for i, (src, dst) in enumerate(head_parts(plane_at(d), source))]

    sent = []
    for d in range(1, planes):
        sent += obs_copies(d, me)
    halos = []
    for way, (row, target) in enumerate(((2 * rows, above), (0, below))):
        for i, (src, dst) in enumerate(own_parts(row)):
            halos.append(remote(src, dst, halo_send.at[way, i], halo_recv.at[way, i], me, target))
    order = sorted(range(1, planes), key=lambda d: -min(d, planes - d))
    for copy in halos + sent:
        copy.start()
    sent_heads = []
    for d in order:
        sent_heads += head_copies(d, me)
    for copy in sent_heads:
        copy.start()

    for copy in local:
        copy.wait()
    for d in range(1, planes):
        for copy in obs_copies(d, plane_at(planes - d)):
            copy.wait_recv()

    row_ids = lax.broadcasted_iota(jnp.int32, (tall, 1), 0)
    col_ids = lax.broadcasted_iota(jnp.int32, (wide, 1), 0)

    def forcing(section, carry):
        for step in range(STEPS):
            cell = cells[section, step : step + 1, :]
            cell_row = cell // total_cols
            cell_col = cell - cell_row * total_cols
            near_row = lax.rem(cell_row - tile * rows + rows + total_rows, total_rows)
            near_col = lax.rem(cell_col - me * cols + LANES + total_cols, total_cols)
            row_hit = near_row == row_ids
            col_hit = jnp.where(near_col == col_ids, 1.0, 0.0).astype(jnp.bfloat16)
            parts = []
            for member in range(2):
                rest = weights[section, step, member : member + 1, :]
                for _ in range(3):
                    part = rest.astype(jnp.bfloat16).astype(jnp.float32)
                    rest = rest - part
                    parts.append(jnp.where(row_hit, part, 0.0).astype(jnp.bfloat16))
            stacked = jnp.concatenate(parts, axis=0)
            got = lax.dot_general(stacked, col_hit, (((1,), (1,)), ((), ())),
                                  preferred_element_type=jnp.float32)
            for member in range(2):
                begin = 3 * member * tall
                force[section, step, member] = (
                    got[begin : begin + tall]
                    + got[begin + tall : begin + 2 * tall]
                    + got[begin + 2 * tall : begin + 3 * tall])
        return carry

    half = planes // 2
    lax.fori_loop(half, planes, forcing, 0, unroll=2)

    for copy in halos:
        copy.wait_recv()

    def activity(shift, j):
        row_tile = lax.rem(tile + shift + tiles, tiles)
        block = lax.rem(first - LANES + j * LANES + total_cols, total_cols) // block_cols
        return mask[(row_tile * rows) // block_rows, block].astype(jnp.float32)

    lane_id = lax.broadcasted_iota(jnp.int32, (rows, LANES), 1)
    row_id = lax.broadcasted_iota(jnp.int32, (rows, LANES), 0)
    act_bands, pair_bands, down_bands = [], [], []
    for band in range(3):
        act_row, pair_row, down_row = [], [], []
        last_row = lax.rem(tile + band - 1 + tiles, tiles) == tiles - 1
        for j in range(wide // LANES):
            here = activity(band - 1, j)
            last_col = lax.rem(first + j * LANES + total_cols, total_cols) == 0
            beside = jnp.where(last_col, 0.0, activity(band - 1, j + 1))
            under = jnp.where(last_row, 0.0, activity(band, j))
            act_row.append(jnp.full((rows, LANES), here, jnp.float32))
            pair_row.append(here * jnp.where(lane_id == LANES - 1, beside, here))
            down_row.append(here * jnp.where(row_id == rows - 1, under, here))
        act_bands.append(jnp.concatenate(act_row, axis=1))
        pair_bands.append(jnp.concatenate(pair_row, axis=1))
        down_bands.append(jnp.concatenate(down_row, axis=1))
    pair_core = pair_bands[1][:, LANES : LANES + cols]
    active = jnp.concatenate(act_bands, axis=0)
    east = ext[1] * jnp.concatenate(pair_bands, axis=0)
    south = ext[2] * jnp.concatenate(down_bands, axis=0)
    west = pltpu.roll(east, 1, 1)
    north = pltpu.roll(south, 1, 0)
    capacity = ext[0]
    inverse = 1.0 / (capacity + east + west + south + north)
    coef[0] = east * inverse
    coef[1] = west * inverse
    coef[2] = south * inverse
    coef[3] = north * inverse
    coef[4] = active * capacity * inverse
    coef[5] = active * inverse

    sub_id = lax.broadcasted_iota(jnp.int32, (1, 8, wide), 1)
    strips = tall // 8

    def stencil(source, i):
        start = pl.multiple_of(i * 8, 8)
        before = pl.multiple_of(jnp.maximum(i - 1, 0) * 8, 8)
        after = pl.multiple_of(jnp.minimum(i + 1, strips - 1) * 8, 8)
        here = source[:, pl.ds(start, 8), :]
        up = jnp.where(sub_id == 0, pltpu.roll(source[:, pl.ds(before, 8), :], 1, 1),
                       pltpu.roll(here, 1, 1))
        down = jnp.where(sub_id == 7, pltpu.roll(source[:, pl.ds(after, 8), :], 7, 1),
                         pltpu.roll(here, 7, 1))
        right = pltpu.roll(here, wide - 1, 2)
        left = pltpu.roll(here, 1, 2)
        strip = pl.ds(start, 8)
        total = (coef[0, strip, :][None] * right + coef[1, strip, :][None] * left
                 + coef[2, strip, :][None] * down + coef[3, strip, :][None] * up)
        return here, total, strip

    def one_step(now, section, step, skip):
        def first_sweep(i, carry):
            here, total, strip = stencil(now, i)
            part = (coef[4, strip, :][None] * here
                    + coef[5, strip, :][None] * force[section, step, :, strip, :])
            rhs[:, strip, :] = part
            mid[:, strip, :] = part + total
            return carry

        def second_sweep(i, carry):
            _, total, strip = stencil(mid, i)
            now[:, strip, :] = rhs[:, strip, :] + total
            return carry

        lax.fori_loop(skip, strips - skip, first_sweep, 0, unroll=True)
        lax.fori_loop(skip, strips - skip, second_sweep, 0, unroll=True)
        saved[section, step] = now[:, rows : 2 * rows, LANES:]

    def start_copy(section, d):
        return remote(saved.at[section, 0, :, :, pl.ds(0, cols)],
                      out_a.at[0, :, :, pl.ds(pl.multiple_of(first, LANES), cols)],
                      start_send.at[d], start_recv.at[d], section, tile)

    def own_start():
        return pltpu.make_async_copy(
            saved.at[me, 0, :, :, pl.ds(0, cols)],
            out_a.at[0, :, :, pl.ds(pl.multiple_of(first, LANES), cols)],
            loc_sem.at[0])

    mids = []
    for phase in range(2):
        now = field.at[phase]

        def one_section(skip, turn, carry):
            section = planes - 1 - phase * half - turn
            for step in reversed(range(STEPS)):
                one_step(now, section, step, skip)
            d = lax.rem(section - me + planes, planes)

            @pl.when(section != me)
            def _():
                start_copy(section, d).start()

            @pl.when(section == me)
            def _():
                own_start().start()

            return carry

        lax.fori_loop(0, half // 2, functools.partial(one_section, 0), 0, unroll=True)
        lax.fori_loop(half // 2, half, functools.partial(one_section, 1), 0, unroll=True)
        if phase == 0:
            core = pl.ds(rows, rows)
            field[1, :, rows : 2 * rows, :] = field[0, :, rows : 2 * rows, :]
            for way, (row, target) in enumerate(((2 * rows, above), (0, below))):
                copy = remote(field.at[0, :, core, :], field.at[1, :, pl.ds(row, rows), :],
                              mid_send.at[way], mid_recv.at[way], me, target)
                copy.start()
                mids.append(copy)
            lax.fori_loop(0, half, forcing, 0)
            for copy in mids:
                copy.wait_recv()


    def sums(turn, carry):
        sens, store_0, store_1, jumps, begins, ends = carry
        d = jnp.where(turn % 2 == 1, (turn + 1) // 2, lax.rem(planes - turn // 2, planes))
        section = plane_at(planes - d)

        @pl.when(turn > 0)
        def _():
            for copy in head_copies(d, section):
                copy.wait_recv()

        for step in range(STEPS):
            a_0 = saved[section, step, 0]
            a_1 = saved[section, step, 1]
            later = head[section, step + 1]
            both = a_0 + a_1
            jump = pltpu.roll(both, edge - 1, 1) - both
            sens = sens + jump[:, :cols] * (pltpu.roll(later, cols - 1, 1) - later)
            here = lane_id == section * STEPS + step
            jumps = jnp.where(here, jump[:, cols - 1 : cols], jumps)
            begins = jnp.where(here, later[:, 0:1], begins)
            ends = jnp.where(here, later[:, cols - 1 : cols], ends)
            change = later - head[section, step]
            store_0 = store_0 + a_0[:, :cols] * change
            store_1 = store_1 + a_1[:, :cols] * change
        return sens, store_0, store_1, jumps, begins, ends

    zero = jnp.zeros((rows, cols), jnp.float32)
    none = jnp.zeros((rows, LANES), jnp.float32)
    sens, store_0, store_1, jumps, begins, ends = lax.fori_loop(
        0, planes, sums, (zero, zero, zero, none, none, none))
    edge_out[...] = begins
    edge_copy = remote(edge_out, edge_in, edge_send, edge_recv, plane_at(planes - 1), tile)
    edge_copy.start()
    cap_core = ext[0, rows : 2 * rows, LANES : LANES + cols]
    tile_lane = lax.broadcasted_iota(jnp.int32, (1, LANES), 1)
    part = jnp.where(tile_lane == 0, jnp.sum(store_0 * cap_core), 0.0)
    part = jnp.where(tile_lane == 1, jnp.sum(store_1 * cap_core), part)

    reduce_sends = []

    def exchange(value, slots, place_here, count, partner, base):
        slots[place_here] = value
        copies = []
        for d in range(1, count):
            plane, row_tile = partner(d)
            copies.append(remote(slots.at[place_here], slots.at[place_here],
                                 red_send.at[base + d], red_recv.at[base + d], plane, row_tile))
        for copy in copies:
            copy.start()
        for d in range(1, count):
            source = lax.rem(place_here + count - d, count)
            plane, row_tile = partner(d)
            remote(slots.at[source], slots.at[source], red_send.at[base + d],
                   red_recv.at[base + d], plane, row_tile).wait_recv()
        reduce_sends.extend(copies)
        return jnp.sum(slots[...], axis=0)

    part = exchange(part, red_b, tile, tiles, lambda d: (me, tile_at(d)), 0)
    part = exchange(part, red_a, me, planes, lambda d: (plane_at(d), tile), tiles)
    out_s[0] = jnp.sum(jnp.where(tile_lane == 0, part, 0.0))
    out_s[1] = jnp.sum(jnp.where(tile_lane == 1, part, 0.0))

    edge_copy.wait_recv()
    last = jnp.sum(jumps * (edge_in[...] - ends), axis=1, keepdims=True)
    col = lax.broadcasted_iota(jnp.int32, (rows, cols), 1)
    out_c[...] = jnp.where(col == cols - 1, last, sens) * pair_core

    own_start().wait()
    for d in range(1, planes):
        source = plane_at(planes - d)
        remote(saved.at[me, 0, :, :, pl.ds(0, cols)],
               out_a.at[0, :, :, pl.ds(pl.multiple_of(source * cols, LANES), cols)],
               start_send.at[d], start_recv.at[d], plane_at(d), tile).wait_recv()
    for d in range(1, planes):
        start_copy(plane_at(d), d).wait_send()
    for copy in sent + halos + sent_heads + mids + reduce_sends + [edge_copy]:
        copy.wait_send()


def solution(mesh):
    planes, tiles = mesh.shape["tm"], mesh.shape["tile"]

    def shards(heads, capacity, cond_row, cond_col, terminal, obs_cell, obs_weight, block_mask):
        rows, total_cols = capacity.shape
        cols = total_cols // planes
        wide, tall, edge = cols + 2 * LANES, 3 * rows, cols + LANES
        observed = obs_cell.shape[2]
        block_rows = rows * tiles // block_mask.shape[0]
        block_cols = total_cols // block_mask.shape[1]
        cfg = (planes, tiles, rows, cols, total_cols, block_rows, block_cols)
        f32 = jnp.float32
        dma = pltpu.SemaphoreType.DMA
        any_spec = pl.BlockSpec(memory_space=pl.ANY)
        out = pl.pallas_call(
            functools.partial(kernel, cfg),
            out_shape=(
                jax.ShapeDtypeStruct((1, 2, rows, total_cols), f32),
                jax.ShapeDtypeStruct((rows, cols), f32),
                jax.ShapeDtypeStruct((2,), f32),
            ),
            in_specs=[any_spec] * 7 + [pl.BlockSpec(memory_space=pltpu.SMEM)],
            out_specs=(any_spec, pl.BlockSpec(memory_space=pltpu.VMEM),
                       pl.BlockSpec(memory_space=pltpu.SMEM)),
            scratch_shapes=[
                pltpu.VMEM((3, tall, wide), f32),
                pltpu.VMEM((2, 2, tall, wide), f32),
                pltpu.VMEM((2, tall, wide), f32),
                pltpu.VMEM((2, tall, wide), f32),
                pltpu.VMEM((6, tall, wide), f32),
                pltpu.VMEM((planes, STEPS, 2, tall, wide), f32),
                pltpu.VMEM((planes, STEPS, observed), jnp.int32),
                pltpu.VMEM((planes, STEPS, 2, observed), f32),
                pltpu.VMEM((planes, 3, rows, cols), f32),
                pltpu.VMEM((planes, STEPS, 2, rows, edge), f32),
                pltpu.VMEM((planes, 1, LANES), f32),
                pltpu.VMEM((tiles, 1, LANES), f32),
                pltpu.VMEM((rows, LANES), f32),
                pltpu.VMEM((rows, LANES), f32),
                dma((16,)),
                dma((2, 12)),
                dma((2, 12)),
                dma((planes, 2)),
                dma((planes, 2)),
                dma((planes, 2)),
                dma((planes, 2)),
                dma((2,)),
                dma((2,)),
                dma((planes,)),
                dma((planes,)),
                dma((planes + tiles,)),
                dma((planes + tiles,)),
                dma(()),
                dma(()),
            ],
            compiler_params=pltpu.CompilerParams(
                collective_id=0, has_side_effects=True, vmem_limit_bytes=67043328
            ),
        )(heads, capacity, cond_row, cond_col, terminal, obs_cell, obs_weight, block_mask)
        return out

    in_specs = (
        P("tm", None, "tile", None),
        P("tile", None),
        P("tile", None),
        P("tile", None),
        P(None, "tile", None),
        P("tm", None, None),
        P("tm", None, None, None),
        P(),
    )
    out_specs = (P("tm", None, "tile", None), P("tile", "tm"), P())
    return jax.shard_map(
        shards, mesh=mesh, in_specs=in_specs, out_specs=out_specs, check_vma=False
    )
```
